512 devices in a mesh: tm: 64 (over z_lo, y, core), space: 8 (over z_hi, x).
Axes of the slice: x: 4, y: 8, z: 8 (z_hi: 2, z_lo: 4; z = z_hi * 4 + z_lo), core: 2. Of those that a mesh axis runs over, the one named last changes fastest.
Arguments:
- queries: bfloat16 [196608, 512], P(('tm', 'space'))
- keys: bfloat16 [196608, 512], P(('tm', 'space'))
- values: bfloat16 [196608, 512], P(('tm', 'space')), may hold values from -6 to 6
- block_mask: int32 [1536, 6, 3], P(('tm', 'space')), may hold values 0 or 1
- tile_counts: int32 [64, 8], P('tm', 'space'), may hold values from 193 to 384, as said below
Outputs:
- attended: bfloat16 [196608, 512], P(('tm', 'space'))
The draws below stay inside these ranges and needn't reach their ends.
Inputs may be any that keep to these rules, and one draw needn't show every extreme that they name: `tile_counts`: at least one tile has all 384 slots live.
All inputs are finite; a program needn't handle non-finite values. No bound on the sum of `block_mask` on one device may be relied on, other than what follows from the above.
Results may differ from the reference program's by a relative error of at most 0.0049.
Values may be sent and summed in bfloat16 or wider, within the bound.
No kernel may reach another device: no remote copies, remote signals or barrier semaphores. Data moves between devices by JAX's collectives and lax.ppermute only.
A program may use at most 128 MiB of HBM per device.

```python
import jax
import jax.numpy as jnp
from jax import lax

HEAD = 128
HEADS = 4
BLK = 128
TOK_DEV = 384
TOKENS = 196608
LOG_TM = 6
N_TM = 64
N_SPACE = 8


def query_key_pair(key):
    base = jax.random.fold_in(key, 7)
    first, second = jax.random.split(base)
    shape = (TOKENS, HEADS * HEAD)
    key_draw = jnp.clip(jax.random.normal(first, shape, jnp.float32), -6.0, 6.0)
    query_draw = jnp.clip(2.5 * jax.random.normal(second, shape, jnp.float32), -15.0, 15.0)
    return (query_draw, key_draw)


def draw_queries(key, part):
    return query_key_pair(key)[0].astype(jnp.bfloat16)


def draw_keys(key, part):
    return query_key_pair(key)[1].astype(jnp.bfloat16)


def draw_tile_counts(key, part):
    first, second = jax.random.split(jax.random.fold_in(key, 11))
    count_draw = TOK_DEV - jax.random.randint(first, (N_TM * N_SPACE,), 0, TOK_DEV // 2)
    chosen = jax.random.randint(second, (), 0, N_TM * N_SPACE)
    flat_ids = jnp.arange(N_TM * N_SPACE, dtype=jnp.int32)
    count_draw = jnp.where(flat_ids == chosen, TOK_DEV, count_draw)
    return count_draw.reshape(N_TM, N_SPACE).astype(jnp.int32)


def plant(values, own_key, least, top_value):
    longest = values.shape.index(max(values.shape))
    spots = []
    for shift in (0, 1):
        where = [jax.random.randint(jax.random.fold_in(own_key, axis), (), 0, length) for axis, length in enumerate(values.shape)]
        where[longest] = (where[longest] + shift) % values.shape[longest]
        spots.append(tuple(where))
    return values.at[spots[0]].set(least).at[spots[1]].set(top_value)


def level_of(key, extent, cuts, least, largest):
    def one(position, shards_of):
        steps = jax.random.uniform(jax.random.fold_in(jax.random.fold_in(key, 6), position), (shards_of,), jnp.float32, least / len(cuts), largest / len(cuts))
        return jnp.repeat(jnp.exp(steps), extent[position] // shards_of).reshape((-1,) + (1,) * (len(extent) - position - 1))

    factor_of = one(*cuts[0])
    for cut in cuts[1:]:
        factor_of = factor_of * one(*cut)
    return factor_of


def scatter_about(own_key, extent, scale, limit, pieces=(), kind=jnp.bfloat16):
    drawn = jax.random.normal(own_key, extent, jnp.float32) * scale
    if len(pieces) > 0:
        drawn = level_of(own_key, extent, pieces, -0.22, 0.18) * drawn
    return jnp.clip(drawn, min=-limit, max=limit).astype(kind)


def setup_inputs(seed: int = 0) -> dict:
    arg_keys = jax.random.split(jax.random.key(seed), 6)
    return {
        "queries": draw_queries(jax.random.fold_in(arg_keys[5], 71), 0),
        "keys": draw_keys(jax.random.fold_in(arg_keys[5], 71), 0),
        "values": scatter_about(arg_keys[2], (TOKENS, HEADS * HEAD), 1.0, 6.0, ((0, 512),)),
        "block_mask": plant((jax.random.randint(arg_keys[3], (TOKENS // BLK, LOG_TM, TOK_DEV // BLK), 0, 2) < 1).astype(jnp.int32), jax.random.fold_in(arg_keys[3], 1), 0, 1),
        "tile_counts": draw_tile_counts(jax.random.fold_in(arg_keys[5], 71), 0),
    }


def reference(queries, keys, values, block_mask, tile_counts):
    width = HEADS * HEAD
    query_g = queries.reshape(N_TM, N_SPACE, TOK_DEV, width)
    key_g = keys.reshape(N_TM, N_SPACE, TOK_DEV, width)
    value_g = values.reshape(N_TM, N_SPACE, TOK_DEV, width)
    mask_g = block_mask.reshape(N_TM, N_SPACE, TOK_DEV // BLK, LOG_TM, TOK_DEV // BLK)
    row_ids = jnp.arange(TOK_DEV, dtype=jnp.int32)
    scale = 1.0 / (HEAD ** 0.5)

    def one_tile(flat):
        group = flat // N_SPACE
        tile = flat % N_SPACE
        key_list = []
        value_list = []
        valid_list = []
        for offset in (-1, 0, 1):
            other = jnp.clip(tile + offset, 0, N_SPACE - 1)
            exists = (tile + offset >= 0) & (tile + offset < N_SPACE)
            key_list.append(key_g[group, other])
            value_list.append(value_g[group, other])
            live = exists & (row_ids < tile_counts[group, other])
            valid_list.append(jnp.broadcast_to(live[None, :], (TOK_DEV, TOK_DEV)))
        for bit_number in range(LOG_TM):
            partner = jnp.bitwise_xor(group, 1 << bit_number)
            key_list.append(key_g[partner, tile])
            value_list.append(value_g[partner, tile])
            blocks = mask_g[group, tile, :, bit_number, :]
            blocks = jnp.repeat(jnp.repeat(blocks, BLK, axis=0), BLK, axis=1)
            live = row_ids < tile_counts[partner, tile]
            valid_list.append((blocks == 1) & live[None, :])
        all_keys = jnp.concatenate(key_list, axis=0).astype(jnp.float32).reshape(-1, HEADS, HEAD)
        all_values = jnp.concatenate(value_list, axis=0).astype(jnp.float32).reshape(-1, HEADS, HEAD)
        valid = jnp.concatenate(valid_list, axis=1)
        query_f = query_g[group, tile].astype(jnp.float32).reshape(TOK_DEV, HEADS, HEAD)
        scores = jnp.einsum('qhe,khe->hqk', query_f, all_keys) * scale
        scores = jnp.where(valid[None], scores, jnp.float32(-1e30))
        top = jnp.max(scores, axis=2, keepdims=True)
        expo = jnp.where(valid[None], jnp.exp(scores - top), jnp.float32(0.0))
        probs = (expo / jnp.sum(expo, axis=2, keepdims=True)).astype(jnp.bfloat16)
        result = jnp.einsum('hqk,khe->qhe', probs.astype(jnp.float32), all_values).reshape(TOK_DEV, width)
        result = jnp.where((row_ids < tile_counts[group, tile])[:, None], result, jnp.float32(0.0))
        return result.astype(jnp.bfloat16)

    tiles = lax.map(one_tile, jnp.arange(N_TM * N_SPACE, dtype=jnp.int32))
    return tiles.reshape(TOKENS, width)
```

```python
import functools

import jax
import jax.numpy as jnp
from jax import lax
from jax.experimental import pallas as pl
from jax.experimental.pallas import tpu as pltpu
from jax.sharding import PartitionSpec as P

HEAD = 128
BLK = 128
LOG2E = 1.4426950408889634
NEG = -1e30


def attend_kernel(kinds, packed, first, last, heads, scal, q_ref, *refs):
    refs = list(refs)
    tiles = []
    width = heads * HEAD
    for whole in packed:
        if whole:
            kv = refs.pop(0)
            tiles.append((kv, kv, width))
        else:
            tiles.append((refs.pop(0), refs.pop(0), 0))
    if not first:
        m_in, l_in, a_in = refs[:3]
        refs = refs[3:]
    if last:
        (out_ref,) = refs
    else:
        m_out, l_out, a_out = refs
    rows = q_ref.shape[0]
    blocks = rows // BLK
    scale = (1.0 / HEAD**0.5) * LOG2E
    lane = lax.broadcasted_iota(jnp.int32, (1, BLK), 1).astype(jnp.float32)

    valid = []
    for kind, (k_ref, _, _) in zip(kinds, tiles):
        if kind == "own":
            count = jnp.full((1, BLK), scal[0], jnp.int32).astype(jnp.float32)
        else:
            tail = k_ref[rows - 16 : rows, 0 : 3 * BLK].astype(jnp.float32)[15:16]
            count = jnp.where(
                tail[:, :BLK] == jnp.inf,
                tail[:, BLK : 2 * BLK] * 128.0 + tail[:, 2 * BLK :],
                jnp.float32(rows),
            )
        per_q = []
        for qb in range(blocks):
            if kind == "own":
                gates = [None] * blocks
            elif kind == "low":
                gates = [scal[1]] * blocks
            elif kind == "high":
                gates = [scal[2]] * blocks
            else:
                base = 3 + (qb * 6 + kind) * blocks
                gates = [scal[base + kb] for kb in range(blocks)]
            row = []
            for kb in range(blocks):
                limit = count - float(kb * BLK)
                if gates[kb] is not None:
                    limit = jnp.where(gates[kb] == 1, limit, jnp.float32(-1.0))
                row.append(jnp.broadcast_to(lane < limit, (BLK, BLK)))
            per_q.append(row)
            if kind in ("own", "low", "high"):
                per_q = [row] * blocks
                break
        valid.append(per_q)

    for h in range(heads):
        hs = slice(h * HEAD, (h + 1) * HEAD)
        q = q_ref[:, hs]
        scores = []
        top = None
        for t, (k_ref, _, _) in enumerate(tiles):
            s = lax.dot_general(
                q, k_ref[:, hs], (((1,), (1,)), ((), ())), preferred_element_type=jnp.float32
            )
            cols = []
            for kb in range(blocks):
                col = jnp.concatenate(
                    [
                        jnp.where(
                            valid[t][qb][kb],
                            s[qb * BLK : (qb + 1) * BLK, kb * BLK : (kb + 1) * BLK],
                            jnp.float32(NEG),
                        )
                        for qb in range(blocks)
                    ],
                    axis=0,
                )
                cols.append(col)
                top = col if top is None else jnp.maximum(top, col)
            scores.append(cols)
        top = jnp.broadcast_to(jnp.max(top, axis=1, keepdims=True), (rows, HEAD))
        if not first:
            m_old = m_in[:, hs]
            top = jnp.maximum(top, m_old)
        top_s = top * scale
        total = None
        acc = None
        if not first:
            alpha = jnp.exp2(m_old * scale - top_s)
            total = l_in[:, hs] * alpha
            acc = a_in[:, hs] * alpha
        for t, (_, v_ref, v_off) in enumerate(tiles):
            probs = []
            for kb in range(blocks):
                p = jnp.exp2(scores[t][kb] * scale - top_s)
                total = p if total is None else total + p
                probs.append(p.astype(jnp.bfloat16))
            part = jnp.dot(
                jnp.concatenate(probs, axis=1),
                v_ref[:, v_off + h * HEAD : v_off + (h + 1) * HEAD],
                preferred_element_type=jnp.float32,
            )
            acc = part if acc is None else acc + part
        if last:
            norm = 1.0 / jnp.sum(total, axis=1, keepdims=True)
            live = lax.broadcasted_iota(jnp.int32, (rows, HEAD), 0) < scal[0]
            out_ref[:, hs] = jnp.where(live, acc * norm, 0.0).astype(out_ref.dtype)
        else:
            m_out[:, hs] = top
            l_out[:, hs] = total
            a_out[:, hs] = acc


def attend(scal, q, tiles, state, last):
    rows, width = q.shape
    heads = width // HEAD
    kinds = tuple(t[0] for t in tiles)
    packed = tuple(len(t) == 2 for t in tiles)
    arrays = [a for t in tiles for a in t[1:]]
    first = state is None
    ins = [scal, q] + arrays + ([] if first else list(state))
    vmem = pl.BlockSpec(memory_space=pltpu.VMEM)
    shape = (rows, width)
    if last:
        out_shape = jax.ShapeDtypeStruct(shape, jnp.bfloat16)
        out_specs = vmem
    else:
        out_shape = [jax.ShapeDtypeStruct(shape, jnp.float32)] * 3
        out_specs = [vmem] * 3
    pairs = rows * rows * heads * len(tiles)
    return pl.pallas_call(
        functools.partial(attend_kernel, kinds, packed, first, last, heads),
        out_shape=out_shape,
        in_specs=[pl.BlockSpec(memory_space=pltpu.SMEM)] + [vmem] * (len(ins) - 1),
        out_specs=out_specs,
        compiler_params=pltpu.CompilerParams(vmem_limit_bytes=40 << 20),
        cost_estimate=pl.CostEstimate(
            flops=4 * pairs * HEAD, transcendentals=pairs, bytes_accessed=len(ins) * 2 * rows * width
        ),
        name="attend_" + "_".join(str(k) for k in kinds),
    )(*ins)


def after(value, *earlier):
    return lax.optimization_barrier((value,) + earlier)[0]


def per_device(queries, keys, values, block_mask, tile_counts):
    rows, width = queries.shape
    tm_size = lax.axis_size("tm")
    space_size = lax.axis_size("space")
    space_index = lax.axis_index("space")
    count = tile_counts.reshape(())

    def partner(value, mask):
        return lax.ppermute(value, "tm", [(i, i ^ mask) for i in range(tm_size)])

    scal = jnp.concatenate(
        [
            jnp.stack(
                [
                    count,
                    (space_index > 0).astype(jnp.int32),
                    (space_index < space_size - 1).astype(jnp.int32),
                ]
            ),
            block_mask.reshape(-1),
        ]
    )
    column = lax.broadcasted_iota(jnp.int32, (rows, width), 1) // HEAD
    row = lax.broadcasted_iota(jnp.int32, (rows, width), 0)
    code = jnp.where(
        column == 0,
        jnp.float32(jnp.inf),
        jnp.where(column == 1, count >> 7, count & 127).astype(jnp.float32),
    ).astype(jnp.bfloat16)
    marked = jnp.where((row == rows - 1) & (count < rows), code, keys)

    up = [(i, i + 1) for i in range(space_size - 1)]
    down = [(i + 1, i) for i in range(space_size - 1)]
    y2_k = partner(marked, 4)
    y1_k = partner(marked, 2)
    both = jnp.concatenate([marked, values], axis=1)
    low = lax.ppermute(both, "space", up)
    high = lax.ppermute(both, "space", down)
    z1 = partner(both, 16)
    y4_k = partner(y2_k, 12)
    y2_v = partner(after(values, y2_k, y1_k), 4)
    z2 = partner(after(both, y2_k), 32)
    y4_v = partner(after(y2_v, y4_k), 12)
    y1_v = partner(after(values, y2_v, y4_k), 2)
    core = partner(after(both, y2_k), 1)

    state = attend(scal, queries, [("own", marked, values), (0, core)], None, False)
    state = attend(
        scal,
        queries,
        [("low", low), ("high", high), (4, z1), (2, y2_k, y2_v)],
        state,
        False,
    )
    return attend(
        scal, queries, [(5, z2), (1, y1_k, y1_v), (3, y4_k, y4_v)], state, True
    )


def solution(mesh):
    placed = (
        P(("tm", "space"), None),
        P(("tm", "space"), None),
        P(("tm", "space"), None),
        P(("tm", "space"), None, None),
        P("tm", "space"),
    )
    return jax.shard_map(
        per_device, mesh=mesh, in_specs=placed, out_specs=P(("tm", "space"), None), check_vma=False
    )
```

```python
import functools

import jax
import jax.numpy as jnp
from jax import lax
from jax.experimental import pallas as pl
from jax.experimental.pallas import tpu as pltpu
from jax.sharding import PartitionSpec as P

HEAD = 128
BLK = 128
LOG2E = 1.4426950408889634
NEG = -1e30


def attend_kernel(kinds, packed, first, last, heads, scal, q_ref, *refs):
    refs = list(refs)
    tiles = []
    width = heads * HEAD
    for whole in packed:
        if whole:
            kv = refs.pop(0)
            tiles.append((kv, kv, width))
        else:
            tiles.append((refs.pop(0), refs.pop(0), 0))
    if not first:
        m_in, l_in, a_in = refs[:3]
        refs = refs[3:]
    if last:
        (out_ref,) = refs
    else:
        m_out, l_out, a_out = refs
    rows = q_ref.shape[0]
    blocks = rows // BLK
    scale = (1.0 / HEAD**0.5) * LOG2E
    lane = lax.broadcasted_iota(jnp.int32, (1, BLK), 1).astype(jnp.float32)

    valid = []
    for kind, (k_ref, _, _) in zip(kinds, tiles):
        if kind == "own":
            count = jnp.full((1, BLK), scal[0], jnp.int32).astype(jnp.float32)
        else:
            tail = k_ref[rows - 16 : rows, 0 : 3 * BLK].astype(jnp.float32)[15:16]
            count = jnp.where(
                tail[:, :BLK] == jnp.inf,
                tail[:, BLK : 2 * BLK] * 128.0 + tail[:, 2 * BLK :],
                jnp.float32(rows),
            )
        per_q = []
        for qb in range(blocks):
            if kind == "own":
                gates = [None] * blocks
            elif kind == "low":
                gates = [scal[1]] * blocks
            elif kind == "high":
                gates = [scal[2]] * blocks
            else:
                base = 3 + (qb * 6 + kind) * blocks
                gates = [scal[base + kb] for kb in range(blocks)]
            row = []
            for kb in range(blocks):
                limit = count - float(kb * BLK)
                if gates[kb] is not None:
                    limit = jnp.where(gates[kb] == 1, limit, jnp.float32(-1.0))
                row.append(jnp.broadcast_to(lane < limit, (BLK, BLK)))
            per_q.append(row)
            if kind in ("own", "low", "high"):
                per_q = [row] * blocks
                break
        valid.append(per_q)

    for h in range(heads):
        hs = slice(h * HEAD, (h + 1) * HEAD)
        q = q_ref[:, hs]
        scores = []
        top = None
        for t, (k_ref, _, _) in enumerate(tiles):
            s = lax.dot_general(
                q, k_ref[:, hs], (((1,), (1,)), ((), ())), preferred_element_type=jnp.float32
            )
            cols = []
            for kb in range(blocks):
                col = jnp.concatenate(
                    [
                        jnp.where(
                            valid[t][qb][kb],
                            s[qb * BLK : (qb + 1) * BLK, kb * BLK : (kb + 1) * BLK],
                            jnp.float32(NEG),
                        )
                        for qb in range(blocks)
                    ],
                    axis=0,
                )
                cols.append(col)
                top = col if top is None else jnp.maximum(top, col)
            scores.append(cols)
        top = jnp.broadcast_to(jnp.max(top, axis=1, keepdims=True), (rows, HEAD))
        if not first:
            m_old = m_in[:, hs]
            top = jnp.maximum(top, m_old)
        top_s = top * scale
        total = None
        acc = None
        if not first:
            alpha = jnp.exp2(m_old * scale - top_s)
            total = l_in[:, hs] * alpha
            acc = a_in[:, hs] * alpha
        for t, (_, v_ref, v_off) in enumerate(tiles):
            probs = []
            for kb in range(blocks):
                p = jnp.exp2(scores[t][kb] * scale - top_s)
                total = p if total is None else total + p
                probs.append(p.astype(jnp.bfloat16))
            part = jnp.dot(
                jnp.concatenate(probs, axis=1),
                v_ref[:, v_off + h * HEAD : v_off + (h + 1) * HEAD],
                preferred_element_type=jnp.float32,
            )
            acc = part if acc is None else acc + part
        if last:
            norm = 1.0 / jnp.sum(total, axis=1, keepdims=True)
            live = lax.broadcasted_iota(jnp.int32, (rows, HEAD), 0) < scal[0]
            out_ref[:, hs] = jnp.where(live, acc * norm, 0.0).astype(out_ref.dtype)
        else:
            m_out[:, hs] = top
            l_out[:, hs] = total
            a_out[:, hs] = acc


def attend(scal, q, tiles, state, last):
    rows, width = q.shape
    heads = width // HEAD
    kinds = tuple(t[0] for t in tiles)
    packed = tuple(len(t) == 2 for t in tiles)
    arrays = [a for t in tiles for a in t[1:]]
    first = state is None
    ins = [scal, q] + arrays + ([] if first else list(state))
    vmem = pl.BlockSpec(memory_space=pltpu.VMEM)
    shape = (rows, width)
    if last:
        out_shape = jax.ShapeDtypeStruct(shape, jnp.bfloat16)
        out_specs = vmem
    else:
        out_shape = [jax.ShapeDtypeStruct(shape, jnp.float32)] * 3
        out_specs = [vmem] * 3
    pairs = rows * rows * heads * len(tiles)
    return pl.pallas_call(
        functools.partial(attend_kernel, kinds, packed, first, last, heads),
        out_shape=out_shape,
        in_specs=[pl.BlockSpec(memory_space=pltpu.SMEM)] + [vmem] * (len(ins) - 1),
        out_specs=out_specs,
        compiler_params=pltpu.CompilerParams(vmem_limit_bytes=40 << 20),
        cost_estimate=pl.CostEstimate(
            flops=4 * pairs * HEAD, transcendentals=pairs, bytes_accessed=len(ins) * 2 * rows * width
        ),
        name="attend_" + "_".join(str(k) for k in kinds),
    )(*ins)


def after(value, *earlier):
    return lax.optimization_barrier((value,) + earlier)[0]


def per_device(queries, keys, values, block_mask, tile_counts):
    rows, width = queries.shape
    tm_size = lax.axis_size("tm")
    space_size = lax.axis_size("space")
    space_index = lax.axis_index("space")
    count = tile_counts.reshape(())

    def partner(value, mask):
        return lax.ppermute(value, "tm", [(i, i ^ mask) for i in range(tm_size)])

    scal = jnp.concatenate(
        [
            jnp.stack(
                [
                    count,
                    (space_index > 0).astype(jnp.int32),
                    (space_index < space_size - 1).astype(jnp.int32),
                ]
            ),
            block_mask.reshape(-1),
        ]
    )
    column = lax.broadcasted_iota(jnp.int32, (rows, width), 1) // HEAD
    row = lax.broadcasted_iota(jnp.int32, (rows, width), 0)
    code = jnp.where(
        column == 0,
        jnp.float32(jnp.inf),
        jnp.where(column == 1, count >> 7, count & 127).astype(jnp.float32),
    ).astype(jnp.bfloat16)
    marked = jnp.where((row == rows - 1) & (count < rows), code, keys)

    up = [(i, i + 1) for i in range(space_size - 1)]
    down = [(i + 1, i) for i in range(space_size - 1)]
    both = jnp.concatenate([marked, values], axis=1)
    y4 = partner(both, 8)
    y2 = partner(both, 4)
    y1 = partner(both, 2)
    z2 = partner(both, 32)
    z1 = partner(both, 16)
    state = attend(scal, queries, [("own", both)], None, False)
    second = after(both, z1, z2, state[0])
    low = lax.ppermute(second, "space", up)
    high = lax.ppermute(second, "space", down)
    state = attend(scal, queries, [(4, z1), (5, z2)], state, False)
    core = partner(after(both, state[0]), 1)
    state = attend(scal, queries, [(3, y4), (2, y2), (1, y1)], state, False)
    return attend(scal, queries, [("low", low), ("high", high), (0, core)], state, True)


def solution(mesh):
    placed = (
        P(("tm", "space"), None),
        P(("tm", "space"), None),
        P(("tm", "space"), None),
        P(("tm", "space"), None, None),
        P("tm", "space"),
    )
    return jax.shard_map(
        per_device, mesh=mesh, in_specs=placed, out_specs=P(("tm", "space"), None), check_vma=False
    )
```

```python
import functools

import jax
import jax.numpy as jnp
from jax import lax
from jax.experimental import pallas as pl
from jax.experimental.pallas import tpu as pltpu
from jax.sharding import PartitionSpec as P

HEAD = 128
BLK = 128
LOG2E = 1.4426950408889634
NEG = -1e30


def attend_kernel(kinds, packed, first, last, heads, scal, q_ref, *refs):
    refs = list(refs)
    tiles = []
    width = heads * HEAD
    for whole in packed:
        if whole:
            kv = refs.pop(0)
            tiles.append((kv, kv, width))
        else:
            tiles.append((refs.pop(0), refs.pop(0), 0))
    if not first:
        m_in, l_in, a_in = refs[:3]
        refs = refs[3:]
    if last:
        (out_ref,) = refs
    else:
        m_out, l_out, a_out = refs
    rows = q_ref.shape[0]
    blocks = rows // BLK
    scale = (1.0 / HEAD**0.5) * LOG2E
    lane = lax.broadcasted_iota(jnp.int32, (1, BLK), 1).astype(jnp.float32)

    valid = []
    for kind, (k_ref, _, _) in zip(kinds, tiles):
        if kind == "own":
            count = jnp.full((1, BLK), scal[0], jnp.int32).astype(jnp.float32)
        else:
            tail = k_ref[rows - 16 : rows, 0 : 3 * BLK].astype(jnp.float32)[15:16]
            count = jnp.where(
                tail[:, :BLK] == jnp.inf,
                tail[:, BLK : 2 * BLK] * 128.0 + tail[:, 2 * BLK :],
                jnp.float32(rows),
            )
        per_q = []
        for qb in range(blocks):
            if kind == "own":
                gates = [None] * blocks
            elif kind == "low":
                gates = [scal[1]] * blocks
            elif kind == "high":
                gates = [scal[2]] * blocks
            else:
                base = 3 + (qb * 6 + kind) * blocks
                gates = [scal[base + kb] for kb in range(blocks)]
            row = []
            for kb in range(blocks):
                limit = count - float(kb * BLK)
                if gates[kb] is not None:
                    limit = jnp.where(gates[kb] == 1, limit, jnp.float32(-1.0))
                row.append(jnp.broadcast_to(lane < limit, (BLK, BLK)))
            per_q.append(row)
            if kind in ("own", "low", "high"):
                per_q = [row] * blocks
                break
        valid.append(per_q)

    def head_scores(h):
        hs = slice(h * HEAD, (h + 1) * HEAD)
        keys = jnp.concatenate([k_ref[:, hs] for k_ref, _, _ in tiles], axis=0)
        return lax.dot_general(
            q_ref[:, hs], keys, (((1,), (1,)), ((), ())), preferred_element_type=jnp.float32
        )

    def head_finish(h, s):
        hs = slice(h * HEAD, (h + 1) * HEAD)
        top = None
        cols = []
        for t in range(len(tiles)):
            for kb in range(blocks):
                at = (t * blocks + kb) * BLK
                col = jnp.concatenate(
                    [
                        jnp.where(
                            valid[t][qb][kb],
                            s[qb * BLK : (qb + 1) * BLK, at : at + BLK],
                            jnp.float32(NEG),
                        )
                        for qb in range(blocks)
                    ],
                    axis=0,
                )
                cols.append(col)
                top = col if top is None else jnp.maximum(top, col)
        top = jnp.broadcast_to(jnp.max(top, axis=1, keepdims=True), (rows, HEAD))
        if not first:
            m_old = m_in[:, hs]
            top = jnp.maximum(top, m_old)
        top_s = top * scale
        probs = [jnp.exp2(col * scale - top_s).astype(jnp.bfloat16) for col in cols]
        vals = []
        for _, v_ref, v_off in tiles:
            v = v_ref[:, v_off + h * HEAD : v_off + (h + 1) * HEAD]
            vals.append(jnp.concatenate([v, jnp.ones_like(v)], axis=1))
        part = jnp.dot(
            jnp.concatenate(probs, axis=1),
            jnp.concatenate(vals, axis=0),
            preferred_element_type=jnp.float32,
        )
        acc, total = part[:, :HEAD], part[:, HEAD:]
        if not first:
            alpha = jnp.exp2(m_old * scale - top_s)
            total = total + l_in[:, hs] * alpha
            acc = acc + a_in[:, hs] * alpha
        if last:
            live = lax.broadcasted_iota(jnp.int32, (rows, HEAD), 0) < scal[0]
            out_ref[:, hs] = jnp.where(live, acc / total, 0.0).astype(out_ref.dtype)
        else:
            m_out[:, hs] = top
            l_out[:, hs] = total
            a_out[:, hs] = acc

    ready = head_scores(0)
    for h in range(heads):
        following = head_scores(h + 1) if h + 1 < heads else None
        head_finish(h, ready)
        ready = following


def attend(scal, q, tiles, state, last):
    rows, width = q.shape
    heads = width // HEAD
    kinds = tuple(t[0] for t in tiles)
    packed = tuple(len(t) == 2 for t in tiles)
    arrays = [a for t in tiles for a in t[1:]]
    first = state is None
    ins = [scal, q] + arrays + ([] if first else list(state))
    vmem = pl.BlockSpec(memory_space=pltpu.VMEM)
    shape = (rows, width)
    if last:
        out_shape = jax.ShapeDtypeStruct(shape, jnp.bfloat16)
        out_specs = vmem
    else:
        out_shape = [jax.ShapeDtypeStruct(shape, jnp.float32)] * 3
        out_specs = [vmem] * 3
    pairs = rows * rows * heads * len(tiles)
    return pl.pallas_call(
        functools.partial(attend_kernel, kinds, packed, first, last, heads),
        out_shape=out_shape,
        in_specs=[pl.BlockSpec(memory_space=pltpu.SMEM)] + [vmem] * (len(ins) - 1),
        out_specs=out_specs,
        compiler_params=pltpu.CompilerParams(vmem_limit_bytes=40 << 20),
        cost_estimate=pl.CostEstimate(
            flops=4 * pairs * HEAD, transcendentals=pairs, bytes_accessed=len(ins) * 2 * rows * width
        ),
        name="attend_" + "_".join(str(k) for k in kinds),
    )(*ins)


def after(value, *earlier):
    return lax.optimization_barrier((value,) + earlier)[0]


def per_device(queries, keys, values, block_mask, tile_counts):
    rows, width = queries.shape
    tm_size = lax.axis_size("tm")
    space_size = lax.axis_size("space")
    space_index = lax.axis_index("space")
    count = tile_counts.reshape(())

    def partner(value, mask):
        return lax.ppermute(value, "tm", [(i, i ^ mask) for i in range(tm_size)])

    scal = jnp.concatenate(
        [
            jnp.stack(
                [
                    count,
                    (space_index > 0).astype(jnp.int32),
                    (space_index < space_size - 1).astype(jnp.int32),
                ]
            ),
            block_mask.reshape(-1),
        ]
    )
    column = lax.broadcasted_iota(jnp.int32, (rows, width), 1) // HEAD
    row = lax.broadcasted_iota(jnp.int32, (rows, width), 0)
    code = jnp.where(
        column == 0,
        jnp.float32(jnp.inf),
        jnp.where(column == 1, count >> 7, count & 127).astype(jnp.float32),
    ).astype(jnp.bfloat16)
    marked = jnp.where((row == rows - 1) & (count < rows), code, keys)

    up = [(i, i + 1) for i in range(space_size - 1)]
    down = [(i + 1, i) for i in range(space_size - 1)]
    both = jnp.concatenate([marked, values], axis=1)
    y2_k = partner(marked, 4)
    y4_v = partner(values, 8)
    y1 = partner(both, 2)
    z2 = partner(both, 32)
    z1 = partner(both, 16)
    core = partner(both, 1)
    state = attend(scal, queries, [("own", both), (0, core)], None, False)
    y4_k = partner(after(y2_k, state[0]), 12)
    y2_v = partner(after(values, y2_k, y4_v, state[0]), 4)
    second = after(both, z1, z2, state[0])
    low = lax.ppermute(second, "space", up)
    high = lax.ppermute(second, "space", down)
    state = attend(scal, queries, [(4, z1), (5, z2)], state, False)
    state = attend(scal, queries, [(1, y1)], state, False)
    state = attend(scal, queries, [(3, y4_k, y4_v), (2, y2_k, y2_v)], state, False)
    return attend(scal, queries, [("low", low), ("high", high)], state, True)


def solution(mesh):
    placed = (
        P(("tm", "space"), None),
        P(("tm", "space"), None),
        P(("tm", "space"), None),
        P(("tm", "space"), None, None),
        P("tm", "space"),
    )
    return jax.shard_map(
        per_device, mesh=mesh, in_specs=placed, out_specs=P(("tm", "space"), None), check_vma=False
    )
```

```python
import functools

import jax
import jax.numpy as jnp
from jax import lax
from jax.experimental import pallas as pl
from jax.experimental.pallas import tpu as pltpu
from jax.sharding import PartitionSpec as P

HEAD = 128
BLK = 128
LOG2E = 1.4426950408889634
NEG = -1e30
TM = ("b5", "b4", "b3", "b2", "b1", "b0")


def attend_kernel(kinds, packed, first, last, heads, scal, q_ref, *refs):
    refs = list(refs)
    tiles = []
    width = heads * HEAD
    for whole in packed:
        if whole:
            kv = refs.pop(0)
            if len(kv.shape) == 3:
                kv = kv.at[scal[3]]
            tiles.append((kv, kv, width))
        else:
            tiles.append((refs.pop(0), refs.pop(0), 0))
    if not first:
        m_in, l_in, a_in = refs[:3]
        refs = refs[3:]
    if last:
        (out_ref,) = refs
    else:
        m_out, l_out, a_out = refs
    rows = q_ref.shape[0]
    blocks = rows // BLK
    scale = (1.0 / HEAD**0.5) * LOG2E
    lane = lax.broadcasted_iota(jnp.int32, (1, BLK), 1).astype(jnp.float32)

    valid = []
    for kind, (k_ref, _, _) in zip(kinds, tiles):
        if kind == "own":
            count = jnp.full((1, BLK), scal[0], jnp.int32).astype(jnp.float32)
        else:
            tail = k_ref[rows - 16 : rows, 0 : 3 * BLK].astype(jnp.float32)[15:16]
            count = jnp.where(
                tail[:, :BLK] == jnp.inf,
                tail[:, BLK : 2 * BLK] * 128.0 + tail[:, 2 * BLK :],
                jnp.float32(rows),
            )
        per_q = []
        for qb in range(blocks):
            if kind == "own":
                gates = [None] * blocks
            elif kind == "low":
                gates = [scal[1]] * blocks
            elif kind == "high":
                gates = [scal[2]] * blocks
            else:
                base = 4 + (qb * 6 + kind) * blocks
                gates = [scal[base + kb] for kb in range(blocks)]
            row = []
            for kb in range(blocks):
                limit = count - float(kb * BLK)
                if gates[kb] is not None:
                    limit = jnp.where(gates[kb] == 1, limit, jnp.float32(-1.0))
                row.append(jnp.broadcast_to(lane < limit, (BLK, BLK)))
            per_q.append(row)
            if kind in ("own", "low", "high"):
                per_q = [row] * blocks
                break
        valid.append(per_q)

    def head_scores(h):
        hs = slice(h * HEAD, (h + 1) * HEAD)
        keys = jnp.concatenate([k_ref[:, hs] for k_ref, _, _ in tiles], axis=0)
        return lax.dot_general(
            q_ref[:, hs], keys, (((1,), (1,)), ((), ())), preferred_element_type=jnp.float32
        )

    def head_finish(h, s):
        hs = slice(h * HEAD, (h + 1) * HEAD)
        top = None
        cols = []
        for t in range(len(tiles)):
            for kb in range(blocks):
                at = (t * blocks + kb) * BLK
                col = jnp.concatenate(
                    [
                        jnp.where(
                            valid[t][qb][kb],
                            s[qb * BLK : (qb + 1) * BLK, at : at + BLK],
                            jnp.float32(NEG),
                        )
                        for qb in range(blocks)
                    ],
                    axis=0,
                )
                cols.append(col)
                top = col if top is None else jnp.maximum(top, col)
        top = jnp.broadcast_to(jnp.max(top, axis=1, keepdims=True), (rows, HEAD))
        if not first:
            m_old = m_in[:, hs]
            top = jnp.maximum(top, m_old)
        top_s = top * scale
        probs = [jnp.exp2(col * scale - top_s).astype(jnp.bfloat16) for col in cols]
        vals = []
        for _, v_ref, v_off in tiles:
            v = v_ref[:, v_off + h * HEAD : v_off + (h + 1) * HEAD]
            vals.append(jnp.concatenate([v, jnp.ones_like(v)], axis=1))
        part = jnp.dot(
            jnp.concatenate(probs, axis=1),
            jnp.concatenate(vals, axis=0),
            preferred_element_type=jnp.float32,
        )
        acc, total = part[:, :HEAD], part[:, HEAD:]
        if not first:
            alpha = jnp.exp2(m_old * scale - top_s)
            total = total + l_in[:, hs] * alpha
            acc = acc + a_in[:, hs] * alpha
        if last:
            live = lax.broadcasted_iota(jnp.int32, (rows, HEAD), 0) < scal[0]
            out_ref[:, hs] = jnp.where(live, acc / total, 0.0).astype(out_ref.dtype)
        else:
            m_out[:, hs] = top
            l_out[:, hs] = total
            a_out[:, hs] = acc

    ready = head_scores(0)
    for h in range(heads):
        following = head_scores(h + 1) if h + 1 < heads else None
        head_finish(h, ready)
        ready = following


def attend(scal, q, tiles, state, last):
    rows, width = q.shape
    heads = width // HEAD
    kinds = tuple(t[0] for t in tiles)
    packed = tuple(len(t) == 2 for t in tiles)
    arrays = [a for t in tiles for a in t[1:]]
    first = state is None
    ins = [scal, q] + arrays + ([] if first else list(state))
    vmem = pl.BlockSpec(memory_space=pltpu.VMEM)
    shape = (rows, width)
    if last:
        out_shape = jax.ShapeDtypeStruct(shape, jnp.bfloat16)
        out_specs = vmem
    else:
        out_shape = [jax.ShapeDtypeStruct(shape, jnp.float32)] * 3
        out_specs = [vmem] * 3
    pairs = rows * rows * heads * len(tiles)
    return pl.pallas_call(
        functools.partial(attend_kernel, kinds, packed, first, last, heads),
        out_shape=out_shape,
        in_specs=[pl.BlockSpec(memory_space=pltpu.SMEM)] + [vmem] * (len(ins) - 1),
        out_specs=out_specs,
        compiler_params=pltpu.CompilerParams(vmem_limit_bytes=40 << 20),
        cost_estimate=pl.CostEstimate(
            flops=4 * pairs * HEAD, transcendentals=pairs, bytes_accessed=len(ins) * 2 * rows * width
        ),
        name="attend_" + "_".join(str(k) for k in kinds),
    )(*ins)


def after(value, *earlier):
    return lax.optimization_barrier((value,) + earlier)[0]


def per_device(queries, keys, values, block_mask, tile_counts):
    rows, width = queries.shape
    tm_size = lax.axis_size(TM)
    space_size = lax.axis_size("space")
    space_index = lax.axis_index("space")
    count = tile_counts.reshape(())

    def partner(value, mask):
        return lax.ppermute(value, TM, [(i, i ^ mask) for i in range(tm_size)])

    scal = jnp.concatenate(
        [
            jnp.stack(
                [
                    count,
                    (space_index > 0).astype(jnp.int32),
                    (space_index < space_size - 1).astype(jnp.int32),
                    1 - lax.axis_index("b0"),
                ]
            ),
            block_mask.reshape(-1),
        ]
    )
    column = lax.broadcasted_iota(jnp.int32, (rows, width), 1) // HEAD
    row = lax.broadcasted_iota(jnp.int32, (rows, width), 0)
    code = jnp.where(
        column == 0,
        jnp.float32(jnp.inf),
        jnp.where(column == 1, count >> 7, count & 127).astype(jnp.float32),
    ).astype(jnp.bfloat16)
    marked = jnp.where((row == rows - 1) & (count < rows), code, keys)

    up = [(i, i + 1) for i in range(space_size - 1)]
    down = [(i + 1, i) for i in range(space_size - 1)]
    both = jnp.concatenate([marked, values], axis=1)
    y2_k = partner(marked, 4)
    y4_v = partner(values, 8)
    y1 = partner(both, 2)
    z2 = partner(both, 32)
    z1 = partner(both, 16)
    state = attend(scal, queries, [("own", both)], None, False)
    own = after(both, state[0])
    core = lax.all_to_all(jnp.stack([own, own]), "b0", 0, 0)
    y4_k = partner(after(y2_k, state[0]), 12)
    y2_v = partner(after(values, y2_k, y4_v, state[0]), 4)
    second = after(both, z1, z2, state[0], core)
    low = lax.ppermute(second, "space", up)
    high = lax.ppermute(second, "space", down)
    state = attend(scal, queries, [(4, z1), (5, z2), (0, core)], state, False)
    state = attend(scal, queries, [(1, y1)], state, False)
    state = attend(scal, queries, [(3, y4_k, y4_v), (2, y2_k, y2_v)], state, False)
    return attend(scal, queries, [("low", low), ("high", high)], state, True)


def solution(mesh):
    bits = jax.sharding.Mesh(
        mesh.devices.reshape((2,) * len(TM) + (mesh.shape["space"],)), TM + ("space",)
    )
    rows = TM + ("space",)
    placed = (
        P(rows, None),
        P(rows, None),
        P(rows, None),
        P(rows, None, None),
        P(TM, "space"),
    )
    return jax.shard_map(
        per_device, mesh=bits, in_specs=placed, out_specs=P(rows, None), check_vma=False
    )
```

```python
import functools

import jax
import jax.numpy as jnp
from jax import lax
from jax.experimental import pallas as pl
from jax.experimental.pallas import tpu as pltpu
from jax.sharding import PartitionSpec as P

HEAD = 128
BLK = 128
LOG2E = 1.4426950408889634
NEG = -1e30
TM = ("b5", "b4", "b3", "b2", "b1", "b0")


def attend_kernel(kinds, packed, first, last, heads, scal, q_ref, *refs):
    refs = list(refs)
    tiles = []
    width = heads * HEAD
    for whole in packed:
        if whole:
            kv = refs.pop(0)
            if len(kv.shape) == 3:
                kv = kv.at[scal[3]]
            tiles.append((kv, kv, width))
        else:
            tiles.append((refs.pop(0), refs.pop(0), 0))
    if not first:
        m_in, l_in, a_in = refs[:3]
        refs = refs[3:]
    if last:
        (out_ref,) = refs
    else:
        m_out, l_out, a_out = refs
    rows = q_ref.shape[0]
    blocks = rows // BLK
    scale = (1.0 / HEAD**0.5) * LOG2E
    lane = lax.broadcasted_iota(jnp.int32, (1, BLK), 1).astype(jnp.float32)

    valid = []
    for kind, (k_ref, _, _) in zip(kinds, tiles):
        if kind == "own":
            count = jnp.full((1, BLK), scal[0], jnp.int32).astype(jnp.float32)
        else:
            tail = k_ref[rows - 16 : rows, 0 : 3 * BLK].astype(jnp.float32)[15:16]
            count = jnp.where(
                tail[:, :BLK] == jnp.inf,
                tail[:, BLK : 2 * BLK] * 128.0 + tail[:, 2 * BLK :],
                jnp.float32(rows),
            )
        per_q = []
        for qb in range(blocks):
            if kind == "own":
                gates = [None] * blocks
            elif kind == "low":
                gates = [scal[1]] * blocks
            elif kind == "high":
                gates = [scal[2]] * blocks
            else:
                base = 4 + (qb * 6 + kind) * blocks
                gates = [scal[base + kb] for kb in range(blocks)]
            row = []
            for kb in range(blocks):
                limit = count - float(kb * BLK)
                if gates[kb] is not None:
                    limit = jnp.where(gates[kb] == 1, limit, jnp.float32(-1.0))
                row.append(jnp.broadcast_to(lane < limit, (BLK, BLK)))
            per_q.append(row)
            if kind in ("own", "low", "high"):
                per_q = [row] * blocks
                break
        valid.append(per_q)

    def head_scores(h):
        hs = slice(h * HEAD, (h + 1) * HEAD)
        keys = jnp.concatenate([k_ref[:, hs] for k_ref, _, _ in tiles], axis=0)
        return lax.dot_general(
            q_ref[:, hs], keys, (((1,), (1,)), ((), ())), preferred_element_type=jnp.float32
        )

    def head_finish(h, s):
        hs = slice(h * HEAD, (h + 1) * HEAD)
        top = None
        cols = []
        for t in range(len(tiles)):
            for kb in range(blocks):
                at = (t * blocks + kb) * BLK
                col = jnp.concatenate(
                    [
                        jnp.where(
                            valid[t][qb][kb],
                            s[qb * BLK : (qb + 1) * BLK, at : at + BLK],
                            jnp.float32(NEG),
                        )
                        for qb in range(blocks)
                    ],
                    axis=0,
                )
                cols.append(col)
                top = col if top is None else jnp.maximum(top, col)
        top = jnp.broadcast_to(jnp.max(top, axis=1, keepdims=True), (rows, HEAD))
        if not first:
            m_old = m_in[:, hs]
            top = jnp.maximum(top, m_old)
        top_s = top * scale
        probs = [jnp.exp2(col * scale - top_s).astype(jnp.bfloat16) for col in cols]
        vals = []
        for _, v_ref, v_off in tiles:
            v = v_ref[:, v_off + h * HEAD : v_off + (h + 1) * HEAD]
            vals.append(jnp.concatenate([v, jnp.ones_like(v)], axis=1))
        part = jnp.dot(
            jnp.concatenate(probs, axis=1),
            jnp.concatenate(vals, axis=0),
            preferred_element_type=jnp.float32,
        )
        acc, total = part[:, :HEAD], part[:, HEAD:]
        if not first:
            alpha = jnp.exp2(m_old * scale - top_s)
            total = total + l_in[:, hs] * alpha
            acc = acc + a_in[:, hs] * alpha
        if last:
            live = lax.broadcasted_iota(jnp.int32, (rows, HEAD), 0) < scal[0]
            out_ref[:, hs] = jnp.where(live, acc / total, 0.0).astype(out_ref.dtype)
        else:
            m_out[:, hs] = top
            l_out[:, hs] = total
            a_out[:, hs] = acc

    ready = head_scores(0)
    for h in range(heads):
        following = head_scores(h + 1) if h + 1 < heads else None
        head_finish(h, ready)
        ready = following


def attend(scal, q, tiles, state, last):
    rows, width = q.shape
    heads = width // HEAD
    kinds = tuple(t[0] for t in tiles)
    packed = tuple(len(t) == 2 for t in tiles)
    arrays = [a for t in tiles for a in t[1:]]
    first = state is None
    ins = [scal, q] + arrays + ([] if first else list(state))
    vmem = pl.BlockSpec(memory_space=pltpu.VMEM)
    shape = (rows, width)
    if last:
        out_shape = jax.ShapeDtypeStruct(shape, jnp.bfloat16)
        out_specs = vmem
    else:
        out_shape = [jax.ShapeDtypeStruct(shape, jnp.float32)] * 3
        out_specs = [vmem] * 3
    pairs = rows * rows * heads * len(tiles)
    return pl.pallas_call(
        functools.partial(attend_kernel, kinds, packed, first, last, heads),
        out_shape=out_shape,
        in_specs=[pl.BlockSpec(memory_space=pltpu.SMEM)] + [vmem] * (len(ins) - 1),
        out_specs=out_specs,
        compiler_params=pltpu.CompilerParams(vmem_limit_bytes=40 << 20),
        cost_estimate=pl.CostEstimate(
            flops=4 * pairs * HEAD, transcendentals=pairs, bytes_accessed=len(ins) * 2 * rows * width
        ),
        name="attend_" + "_".join(str(k) for k in kinds),
    )(*ins)


def after(value, *earlier):
    return lax.optimization_barrier((value,) + earlier)[0]


def per_device(queries, keys, values, block_mask, tile_counts):
    rows, width = queries.shape
    tm_size = lax.axis_size(TM)
    space_size = lax.axis_size("space")
    space_index = lax.axis_index("space")
    count = tile_counts.reshape(())

    def partner(value, mask):
        return lax.ppermute(value, TM, [(i, i ^ mask) for i in range(tm_size)])

    scal = jnp.concatenate(
        [
            jnp.stack(
                [
                    count,
                    (space_index > 0).astype(jnp.int32),
                    (space_index < space_size - 1).astype(jnp.int32),
                    1 - lax.axis_index("b0"),
                ]
            ),
            block_mask.reshape(-1),
        ]
    )
    column = lax.broadcasted_iota(jnp.int32, (rows, width), 1) // HEAD
    row = lax.broadcasted_iota(jnp.int32, (rows, width), 0)
    code = jnp.where(
        column == 0,
        jnp.float32(jnp.inf),
        jnp.where(column == 1, count >> 7, count & 127).astype(jnp.float32),
    ).astype(jnp.bfloat16)
    marked = jnp.where((row == rows - 1) & (count < rows), code, keys)

    up = [(i, i + 1) for i in range(space_size - 1)]
    down = [(i + 1, i) for i in range(space_size - 1)]
    both = jnp.concatenate([marked, values], axis=1)
    y2_k = partner(marked, 4)
    y4_v = partner(values, 8)
    y1 = partner(both, 2)
    z2 = partner(both, 32)
    z1 = partner(both, 16)
    state = attend(scal, queries, [("own", both)], None, False)
    own = after(both, state[0])
    core = lax.all_to_all(jnp.stack([own, own]), "b0", 0, 0)
    y4_k = partner(after(y2_k, state[0]), 12)
    y2_v = partner(after(values, y2_k, y4_v, state[0]), 4)
    second = after(both, z2, z1, state[0], core)
    low = lax.ppermute(second, "space", up)
    high = lax.ppermute(second, "space", down)
    state = attend(scal, queries, [(5, z2), (4, z1), (0, core)], state, False)
    state = attend(scal, queries, [(1, y1)], state, False)
    state = attend(scal, queries, [(3, y4_k, y4_v)], state, False)
    state = attend(scal, queries, [(2, y2_k, y2_v)], state, False)
    return attend(scal, queries, [("high", high), ("low", low)], state, True)


def solution(mesh):
    bits = jax.sharding.Mesh(
        mesh.devices.reshape((2,) * len(TM) + (mesh.shape["space"],)), TM + ("space",)
    )
    rows = TM + ("space",)
    placed = (
        P(rows, None),
        P(rows, None),
        P(rows, None),
        P(rows, None, None),
        P(TM, "space"),
    )
    return jax.shard_map(
        per_device, mesh=bits, in_specs=placed, out_specs=P(rows, None), check_vma=False
    )
```

```python
import functools

import jax
import jax.numpy as jnp
from jax import lax
from jax.experimental import pallas as pl
from jax.experimental.pallas import tpu as pltpu
from jax.sharding import PartitionSpec as P

HEAD = 128
BLK = 128
LOG2E = 1.4426950408889634
NEG = -1e30
TM = ("b5", "b4", "b3", "b2", "b1", "b0")


def attend_kernel(kinds, packed, first, last, heads, scal, q_ref, *refs):
    refs = list(refs)
    tiles = []
    width = heads * HEAD
    for whole in packed:
        if whole:
            kv = refs.pop(0)
            if len(kv.shape) == 3:
                kv = kv.at[scal[3]]
            tiles.append((kv, kv, width))
        else:
            tiles.append((refs.pop(0), refs.pop(0), 0))
    if not first:
        m_in, l_in, a_in = refs[:3]
        refs = refs[3:]
    if last:
        (out_ref,) = refs
    else:
        m_out, l_out, a_out = refs
    rows = q_ref.shape[0]
    blocks = rows // BLK
    scale = (1.0 / HEAD**0.5) * LOG2E
    lane = lax.broadcasted_iota(jnp.int32, (1, BLK), 1).astype(jnp.float32)

    valid = []
    for kind, (k_ref, _, _) in zip(kinds, tiles):
        if kind == "own":
            count = jnp.full((1, BLK), scal[0], jnp.int32).astype(jnp.float32)
        else:
            tail = k_ref[rows - 16 : rows, 0 : 3 * BLK].astype(jnp.float32)[15:16]
            count = jnp.where(
                tail[:, :BLK] == jnp.inf,
                tail[:, BLK : 2 * BLK] * 128.0 + tail[:, 2 * BLK :],
                jnp.float32(rows),
            )
        per_q = []
        for qb in range(blocks):
            if kind == "own":
                gates = [None] * blocks
            elif kind == "low":
                gates = [scal[1]] * blocks
            elif kind == "high":
                gates = [scal[2]] * blocks
            else:
                base = 4 + (qb * 6 + kind) * blocks
                gates = [scal[base + kb] for kb in range(blocks)]
            row = []
            for kb in range(blocks):
                limit = count - float(kb * BLK)
                if gates[kb] is not None:
                    limit = jnp.where(gates[kb] == 1, limit, jnp.float32(-1.0))
                row.append(jnp.broadcast_to(lane < limit, (BLK, BLK)))
            per_q.append(row)
            if kind in ("own", "low", "high"):
                per_q = [row] * blocks
                break
        valid.append(per_q)

    def head_scores(h):
        hs = slice(h * HEAD, (h + 1) * HEAD)
        keys = jnp.concatenate([k_ref[:, hs] for k_ref, _, _ in tiles], axis=0)
        return lax.dot_general(
            q_ref[:, hs], keys, (((1,), (1,)), ((), ())), preferred_element_type=jnp.float32
        )

    def head_finish(h, s):
        hs = slice(h * HEAD, (h + 1) * HEAD)
        top = None
        cols = []
        for t in range(len(tiles)):
            for kb in range(blocks):
                at = (t * blocks + kb) * BLK
                col = jnp.concatenate(
                    [
                        jnp.where(
                            valid[t][qb][kb],
                            s[qb * BLK : (qb + 1) * BLK, at : at + BLK],
                            jnp.float32(NEG),
                        )
                        for qb in range(blocks)
                    ],
                    axis=0,
                )
                cols.append(col)
                top = col if top is None else jnp.maximum(top, col)
        top = jnp.broadcast_to(jnp.max(top, axis=1, keepdims=True), (rows, HEAD))
        if not first:
            m_old = m_in[:, hs]
            top = jnp.maximum(top, m_old)
        top_s = top * scale
        probs = [jnp.exp2(col * scale - top_s).astype(jnp.bfloat16) for col in cols]
        vals = []
        for _, v_ref, v_off in tiles:
            v = v_ref[:, v_off + h * HEAD : v_off + (h + 1) * HEAD]
            vals.append(jnp.concatenate([v, jnp.ones_like(v)], axis=1))
        part = jnp.dot(
            jnp.concatenate(probs, axis=1),
            jnp.concatenate(vals, axis=0),
            preferred_element_type=jnp.float32,
        )
        acc, total = part[:, :HEAD], part[:, HEAD:]
        if not first:
            alpha = jnp.exp2(m_old * scale - top_s)
            total = total + l_in[:, hs] * alpha
            acc = acc + a_in[:, hs] * alpha
        if last:
            live = lax.broadcasted_iota(jnp.int32, (rows, HEAD), 0) < scal[0]
            out_ref[:, hs] = jnp.where(live, acc / total, 0.0).astype(out_ref.dtype)
        else:
            m_out[:, hs] = top
            l_out[:, hs] = total
            a_out[:, hs] = acc

    ready = head_scores(0)
    for h in range(heads):
        following = head_scores(h + 1) if h + 1 < heads else None
        head_finish(h, ready)
        ready = following


def attend(scal, q, tiles, state, last):
    rows, width = q.shape
    heads = width // HEAD
    kinds = tuple(t[0] for t in tiles)
    packed = tuple(len(t) == 2 for t in tiles)
    arrays = [a for t in tiles for a in t[1:]]
    first = state is None
    ins = [scal, q] + arrays + ([] if first else list(state))
    vmem = pl.BlockSpec(memory_space=pltpu.VMEM)
    shape = (rows, width)
    if last:
        out_shape = jax.ShapeDtypeStruct(shape, jnp.bfloat16)
        out_specs = vmem
    else:
        out_shape = [jax.ShapeDtypeStruct(shape, jnp.float32)] * 3
        out_specs = [vmem] * 3
    pairs = rows * rows * heads * len(tiles)
    return pl.pallas_call(
        functools.partial(attend_kernel, kinds, packed, first, last, heads),
        out_shape=out_shape,
        in_specs=[pl.BlockSpec(memory_space=pltpu.SMEM)] + [vmem] * (len(ins) - 1),
        out_specs=out_specs,
        compiler_params=pltpu.CompilerParams(vmem_limit_bytes=40 << 20),
        cost_estimate=pl.CostEstimate(
            flops=4 * pairs * HEAD, transcendentals=pairs, bytes_accessed=len(ins) * 2 * rows * width
        ),
        name="attend_" + "_".join(str(k) for k in kinds),
    )(*ins)


def after(value, *earlier):
    return lax.optimization_barrier((value,) + earlier)[0]


def per_device(queries, keys, values, block_mask, tile_counts):
    rows, width = queries.shape
    tm_size = lax.axis_size(TM)
    space_size = lax.axis_size("space")
    space_index = lax.axis_index("space")
    count = tile_counts.reshape(())

    def partner(value, mask):
        return lax.ppermute(value, TM, [(i, i ^ mask) for i in range(tm_size)])

    scal = jnp.concatenate(
        [
            jnp.stack(
                [
                    count,
                    (space_index > 0).astype(jnp.int32),
                    (space_index < space_size - 1).astype(jnp.int32),
                    1 - lax.axis_index("b0"),
                ]
            ),
            block_mask.reshape(-1),
        ]
    )
    column = lax.broadcasted_iota(jnp.int32, (1, width), 1) // HEAD
    code = jnp.where(
        column == 0,
        jnp.float32(jnp.inf),
        jnp.where(column == 1, count >> 7, count & 127).astype(jnp.float32),
    ).astype(jnp.bfloat16)
    end = jnp.where(count < rows, code, keys[rows - 1 :])
    marked = lax.dynamic_update_slice(keys, end, (rows - 1, 0))

    up = [(i, i + 1) for i in range(space_size - 1)]
    down = [(i + 1, i) for i in range(space_size - 1)]
    both = lax.dynamic_update_slice(
        jnp.concatenate([keys, values], axis=1), end, (rows - 1, 0)
    )
    y2_k = partner(marked, 4)
    y4_v = partner(values, 8)
    y1 = partner(both, 2)
    z2 = partner(both, 32)
    z1 = partner(both, 16)
    state = attend(scal, queries, [("own", both)], None, False)
    own = after(both, state[0])
    core = lax.all_to_all(jnp.stack([own, own]), "b0", 0, 0)
    y4_k = partner(after(y2_k, state[0]), 12)
    y2_v = partner(after(values, y2_k, y4_v, state[0]), 4)
    second = after(both, z2, z1, state[0], core)
    low = lax.ppermute(second, "space", up)
    high = lax.ppermute(second, "space", down)
    state = attend(scal, queries, [(5, z2), (4, z1), (0, core)], state, False)
    state = attend(scal, queries, [(1, y1)], state, False)
    state = attend(scal, queries, [(3, y4_k, y4_v)], state, False)
    state = attend(scal, queries, [(2, y2_k, y2_v)], state, False)
    return attend(scal, queries, [("high", high), ("low", low)], state, True)


def solution(mesh):
    bits = jax.sharding.Mesh(
        mesh.devices.reshape((2,) * len(TM) + (mesh.shape["space"],)), TM + ("space",)
    )
    rows = TM + ("space",)
    placed = (
        P(rows, None),
        P(rows, None),
        P(rows, None),
        P(rows, None, None),
        P(TM, "space"),
    )
    return jax.shard_map(
        per_device, mesh=bits, in_specs=placed, out_specs=P(rows, None), check_vma=False
    )
```
